256 devices in a mesh: enc: 16 (over z_hi, x), dec: 8 (over y, core), grp: 2 (over z_lo).
Axes of the slice: x: 4, y: 4, z: 8 (z_hi: 4, z_lo: 2; z = z_hi * 2 + z_lo), core: 2. Of those that a mesh axis runs over, the one named last changes fastest.
Arguments:
- images: bfloat16 [256, 4, 32, 1280], P(('enc', 'dec', 'grp')), may hold values from -6 to 6
- ln_gain: float32 [1280], replicated, may hold values from 0.1 to 1.9
- ln_bias: float32 [1280], replicated, may hold values from -3 to 3
- fc1_weight: bfloat16 [5120, 1280], P('enc'), may hold values from -0.15625 to 0.15625
- fc1_bias: float32 [5120], P('enc'), may hold values from -3 to 3
- fc2_weight: bfloat16 [5120, 1280], P('enc'), may hold values from -0.078125 to 0.078125
- fc2_bias: float32 [1280], replicated, may hold values from -3 to 3
- key_weight: bfloat16 [1280, 512], replicated, may hold values from -0.15625 to 0.15625
- value_weight: bfloat16 [1280, 512], replicated, may hold values from -0.15625 to 0.15625
- text: bfloat16 [64, 128, 8192], P(('enc', 'grp')), may hold values from -6 to 6
- query_weight: bfloat16 [8192, 4096], P('enc', 'dec'), may hold values from -0.0625 to 0.0625
- tiles: int32 [16, 8, 2], replicated, may hold values from 1 to 4, as said below
- links: int32 [64, 8], P(('enc', 'grp')), may hold values from 0 to 1, as said below
- lengths: int32 [64], P(('enc', 'grp')), may hold values from 1 to 128
- state_grads: bfloat16 [256, 4, 32, 1280], P(('enc', 'dec', 'grp')), may hold values from -0.125 to 0.125
Outputs:
- context: bfloat16 [64, 128, 4096], P(('enc', 'grp'), None, 'dec')
- fc1_grad: float32 [5120, 1280], P(('enc', 'dec', 'grp'))
- fc2_grad: float32 [5120, 1280], P(('enc', 'dec', 'grp'))
The draws below stay inside these ranges and needn't reach their ends.
Inputs may be any that keep to these rules, and one draw needn't show every extreme that they name: The 16 images that share their last two indices have 40 tiles together, and one of them has 4. `links`: every text is linked to at least one image.
All inputs are finite; a program needn't handle non-finite values.
Results may differ from the reference program's by a relative error of at most 0.017.
Values may be sent and summed in bfloat16 or wider, within the bound.
No kernel may reach another device: no remote copies, remote signals or barrier semaphores. Data moves between devices by JAX's collectives and lax.ppermute only.
A program may use at most 128 MiB of HBM per device.

```python
import jax
import jax.numpy as jnp
from jax import lax

DV = 1280
FF = 5120
DT = 8192
HEADS = 32
KV_HEADS = 4
HD = 128
TXT = 128
TILES = 4
PATCH = 32
SAMP = 2
IMAGES = 256
TEXTS = 64
N_ENC = 16
N_DEC = 8
N_GRP = 2


def draw_tiles(key, part):
    groups = N_DEC * N_GRP
    group_keys = jax.random.split(jax.random.fold_in(key, 11), groups)

    def one_group(group_key):
        first_key, second_key = jax.random.split(group_key)
        shuffled = jax.random.permutation(first_key, 3 * (N_ENC - 1))
        chosen = (shuffled < 3 * N_ENC // 2 - 3).astype(jnp.int32)
        others = jnp.sum(chosen.reshape(N_ENC - 1, 3), axis=1)
        forced = jax.random.randint(second_key, (), 0, N_ENC)
        index = jnp.arange(N_ENC)
        earlier = jnp.take(others, jnp.clip(index, 0, N_ENC - 2))
        later = jnp.take(others, jnp.clip(index - 1, 0, N_ENC - 2))
        extra = jnp.where(index < forced, earlier, jnp.where(index == forced, 3, later))
        return 1 + extra
    columns = jax.vmap(one_group)(group_keys)
    return columns.T.reshape(N_ENC, N_DEC, N_GRP).astype(jnp.int32)


def draw_links(key, part):
    first_key, second_key = jax.random.split(jax.random.fold_in(key, 23))
    coins = jax.random.randint(first_key, (TEXTS, N_DEC), 0, 5)
    chosen = jax.random.randint(second_key, (TEXTS, 1), 0, N_DEC)
    column = jnp.arange(N_DEC)[None, :]
    return jnp.where((coins < 2) | (column == chosen), 1, 0).astype(jnp.int32)


def with_ends(array, rng, least, high):
    extent = array.shape
    index_at = [jax.random.randint(jax.random.fold_in(rng, axis), (), 0, extent[axis]) for axis in range(len(extent))]
    array = array.at[tuple(index_at)].set(least)
    longest = extent.index(max(extent))
    index_at[longest] = (index_at[longest] + 1) % extent[longest]
    return array.at[tuple(index_at)].set(high)


def steps_of(rng, extent, shards, smallest, largest):
    def one(position, shards_of):
        draws = jax.random.uniform(jax.random.fold_in(jax.random.fold_in(rng, 6), position), (shards_of,), jnp.float32, smallest / len(shards), largest / len(shards))
        return jnp.repeat(jnp.exp(draws), extent[position] // shards_of).reshape((-1,) + (1,) * (len(extent) - position - 1))

    level = one(*shards[0])
    for cut in shards[1:]:
        level = level * one(*cut)
    return level


def normal_values(own_key, shape, scale, bound, cuts=(), kind=jnp.bfloat16):
    entries = scale * jax.random.normal(own_key, shape, jnp.float32)
    if cuts:
        entries = entries * steps_of(own_key, shape, cuts, -0.22, 0.18)
    return jnp.clip(entries, -bound, bound).astype(kind)


def setup_inputs(seed: int = 0) -> dict:
    streams_of = jax.random.split(jax.random.key(seed), 16)
    images = normal_values(streams_of[0], (IMAGES, TILES, PATCH, DV), 1.0, 6.0, ((0, 256),))
    ln_gain = jnp.clip(1.0 + 0.18 * jax.random.normal(streams_of[1], (DV,), jnp.float32), 0.1, 1.9)
    ln_bias = normal_values(streams_of[2], (DV,), 0.5, 3.0, (), jnp.float32)
    fc1_weight = normal_values(streams_of[3], (FF, DV), DV ** -0.5, 0.15625, ((0, 16),))
    fc1_bias = normal_values(streams_of[4], (FF,), 0.5, 3.0, ((0, 16),), jnp.float32)
    fc2_weight = normal_values(streams_of[5], (FF, DV), FF ** -0.5, 0.078125, ((0, 16),))
    fc2_bias = normal_values(streams_of[6], (DV,), 0.5, 3.0, (), jnp.float32)
    key_weight = normal_values(streams_of[7], (DV, KV_HEADS * HD), DV ** -0.5, 0.15625)
    value_weight = normal_values(streams_of[8], (DV, KV_HEADS * HD), DV ** -0.5, 0.15625)
    text = normal_values(streams_of[9], (TEXTS, TXT, DT), 1.0, 6.0, ((0, 32),))
    query_weight = normal_values(streams_of[10], (DT, HEADS * HD), DT ** -0.5, 0.0625, ((0, 16), (1, 8)))
    tiles = draw_tiles(jax.random.fold_in(streams_of[15], 71), 0)
    links = draw_links(jax.random.fold_in(streams_of[15], 71), 0)
    lengths = with_ends(jax.random.randint(streams_of[13], (TEXTS,), 1, TXT + 1), jax.random.fold_in(streams_of[13], 1), 1, TXT).astype(jnp.int32)
    state_grads = normal_values(streams_of[14], (IMAGES, TILES, PATCH, DV), 0.02, 0.125, ((0, 256),))
    return dict(images=images, ln_gain=ln_gain, ln_bias=ln_bias, fc1_weight=fc1_weight, fc1_bias=fc1_bias, fc2_weight=fc2_weight, fc2_bias=fc2_bias, key_weight=key_weight, value_weight=value_weight, text=text, query_weight=query_weight, tiles=tiles, links=links, lengths=lengths, state_grads=state_grads)


EPSILON = 1e-06

def normalize_layer(values, gain, shift):
    middle = lax.optimization_barrier(jnp.mean(values, axis=-1, keepdims=True))
    centered = values - middle
    spread = lax.optimization_barrier(jnp.mean(centered * centered, axis=-1, keepdims=True))
    return centered * lax.rsqrt(spread + EPSILON) * gain + shift

def normalize_heads(values):
    return values * lax.rsqrt(lax.optimization_barrier(jnp.mean(values * values, axis=-1, keepdims=True)) + EPSILON)

def gelu_slope(values):
    return 0.5 * (1.0 + lax.erf(values * 0.7071067811865476)) + values * jnp.exp(-0.5 * values * values) * 0.3989422804014327

def reference(images, ln_gain, ln_bias, fc1_weight, fc1_bias, fc2_weight, fc2_bias, key_weight, value_weight, text, query_weight, tiles, links, lengths, state_grads):
    img_rows = TILES * PATCH
    per_group = HEADS // KV_HEADS
    block_width = FF // N_ENC
    flat_rows = images.reshape(IMAGES * img_rows, DV)
    normed = normalize_layer(flat_rows.astype(jnp.float32), ln_gain, ln_bias).astype(jnp.bfloat16)
    pre = lax.dot_general(normed, fc1_weight, (((1,), (1,)), ((), ())), preferred_element_type=jnp.float32) + fc1_bias
    hidden = jax.nn.gelu(pre, approximate=False).astype(jnp.bfloat16)

    def add_block(block, total):
        start = (block * block_width).astype(jnp.int32)
        part = jnp.dot(lax.dynamic_slice_in_dim(hidden, start, block_width, 1), lax.dynamic_slice_in_dim(fc2_weight, start, block_width, 0), preferred_element_type=jnp.float32)
        rounded = lax.optimization_barrier(part.astype(jnp.bfloat16))
        return total + rounded.astype(jnp.float32)
    partial_sum = lax.fori_loop(0, N_ENC, add_block, jnp.zeros((IMAGES * img_rows, DV), jnp.float32))
    states = (flat_rows.astype(jnp.float32) + partial_sum + fc2_bias).astype(jnp.bfloat16)
    key_raw = jnp.dot(states, key_weight, preferred_element_type=jnp.float32).reshape(IMAGES * img_rows, KV_HEADS, HD)
    keys = normalize_heads(key_raw).astype(jnp.bfloat16)
    values = jnp.dot(states, value_weight, preferred_element_type=jnp.float32).astype(jnp.bfloat16).reshape(IMAGES * img_rows, KV_HEADS, HD)
    keys = keys.reshape(N_ENC, N_DEC, N_GRP, img_rows, KV_HEADS, HD).transpose(0, 2, 4, 1, 3, 5).reshape(N_ENC * N_GRP, KV_HEADS, N_DEC * img_rows, HD)
    values = values.reshape(N_ENC, N_DEC, N_GRP, img_rows, KV_HEADS, HD).transpose(0, 2, 4, 1, 3, 5).reshape(N_ENC * N_GRP, KV_HEADS, N_DEC * img_rows, HD)
    group_tiles = tiles.transpose(0, 2, 1)
    live_keys = (jnp.arange(TILES)[None, None, None, :] < group_tiles[..., None]).astype(jnp.int32)
    live_keys = jnp.broadcast_to(live_keys[..., None], (N_ENC, N_GRP, N_DEC, TILES, PATCH)).reshape(N_ENC * N_GRP, N_DEC, img_rows)
    query_raw = jnp.dot(text.reshape(TEXTS * TXT, DT), query_weight, preferred_element_type=jnp.float32).reshape(TEXTS, TXT, HEADS, HD)
    queries = normalize_heads(query_raw).astype(jnp.bfloat16).reshape(N_ENC * N_GRP, SAMP, TXT, KV_HEADS, per_group, HD)
    group_links = links.reshape(N_ENC * N_GRP, SAMP, N_DEC)
    group_lengths = lengths.reshape(N_ENC * N_GRP, SAMP)

    def attend(inputs):
        group_queries, group_keys, group_values, group_live, link_rows, length_rows = inputs
        allowed = (link_rows[:, :, None] * group_live[None, :, :]).reshape(SAMP, N_DEC * img_rows) > 0
        scores = jnp.einsum('sqghd,gkd->sghqk', group_queries.astype(jnp.float32), group_keys.astype(jnp.float32)) * HD ** (-0.5)
        weights = jnp.where(allowed[:, None, None, None, :], jnp.exp(scores), 0.0)
        probs = (weights / lax.optimization_barrier(jnp.sum(weights, axis=-1, keepdims=True))).astype(jnp.bfloat16)
        mixed = jnp.einsum('sghqk,gkd->sqghd', probs.astype(jnp.float32), group_values.astype(jnp.float32))
        valid = jnp.arange(TXT)[None, :] < length_rows[:, None]
        mixed = jnp.where(valid[:, :, None, None, None], mixed, 0.0)
        return mixed.reshape(SAMP, TXT, HEADS * HD).astype(jnp.bfloat16)
    context = lax.map(attend, (queries, keys, values, live_keys, group_links, group_lengths)).reshape(TEXTS, TXT, HEADS * HD)
    live_rows = jnp.arange(TILES)[None, :] < tiles.reshape(IMAGES)[:, None]
    live_rows = jnp.broadcast_to(live_rows[:, :, None], (IMAGES, TILES, PATCH)).reshape(IMAGES * img_rows, 1)
    cotangent = jnp.where(live_rows, state_grads.reshape(IMAGES * img_rows, DV), jnp.zeros((), state_grads.dtype))
    hidden_grad = lax.dot_general(cotangent, fc2_weight, (((1,), (1,)), ((), ())), preferred_element_type=jnp.float32)
    fc2_grad = lax.dot_general(hidden, cotangent, (((0,), (0,)), ((), ())), preferred_element_type=jnp.float32)
    pre_grad = (hidden_grad * gelu_slope(pre)).astype(jnp.bfloat16)
    fc1_grad = lax.dot_general(pre_grad, normed, (((0,), (0,)), ((), ())), preferred_element_type=jnp.float32)
    return (context, fc1_grad, fc2_grad)
```

```python
import jax
import jax.numpy as jnp
from jax import lax
from jax.sharding import Mesh
from jax.sharding import PartitionSpec as P

HEADS = 32
KV_HEADS = 4
HD = 128
EPSILON = 1e-06
F32 = jnp.float32
BF16 = jnp.bfloat16


def pull(array, axis, step):
    n = lax.axis_size(axis)
    return lax.ppermute(array, axis, [((i + step) % n, i) for i in range(n)])


def push(array, axis, step):
    n = lax.axis_size(axis)
    return lax.ppermute(array, axis, [(i, (i + step) % n) for i in range(n)])


def gather_rel(array, axis):
    return jnp.concatenate(
        [array] + [pull(array, axis, j) for j in range(1, lax.axis_size(axis))], axis=0
    )


def scatter_rel(blocks, axis):
    total = blocks[0].astype(F32)
    for j in range(1, lax.axis_size(axis)):
        total = total + push(blocks[j].astype(BF16), axis, j).astype(F32)
    return total


def normalize_layer(values, gain, shift):
    middle = jnp.mean(values, axis=-1, keepdims=True)
    centered = values - middle
    spread = jnp.mean(centered * centered, axis=-1, keepdims=True)
    return centered * lax.rsqrt(spread + EPSILON) * gain + shift


def normalize_heads(values):
    return values * lax.rsqrt(jnp.mean(values * values, axis=-1, keepdims=True) + EPSILON)


def three_terms(column):
    first = lax.reduce_precision(column, 8, 7)
    second = lax.reduce_precision(column - first, 8, 7)
    third = column - first - second
    lane = lax.broadcasted_iota(jnp.int32, (column.shape[0], 128), 1)
    return jnp.where(
        lane == 0, first, jnp.where(lane == 1, second, jnp.where(lane == 2, third, 0.0))
    ).astype(BF16)


def gather_weight(piece):
    piece = gather_rel(piece, "zh")
    piece = gather_rel(piece, "y")
    return gather_rel(piece, "core")


def scatter_grad(grad):
    rows, width = grad.shape
    grad = scatter_rel(list(grad.reshape(2, rows // 2, width)), "core")
    grad = scatter_rel(list(grad.reshape(4, rows // 8, width)), "y")
    grad = scatter_rel(list(grad.reshape(4, rows // 32, width)), "zh")
    half = rows // 64
    own = lax.axis_index("grp") * half
    mine = lax.dynamic_slice_in_dim(grad, own, half, 0)
    theirs = lax.dynamic_slice_in_dim(grad, half - own, half, 0)
    return mine + push(theirs.astype(BF16), "grp", 1).astype(F32)


def on_device(
    images,
    ln_gain,
    ln_bias,
    fc1_weight,
    fc1_bias,
    fc2_weight,
    fc2_bias,
    key_weight,
    value_weight,
    text,
    query_weight,
    tiles,
    links,
    lengths,
    state_grads,
):
    zh, x, y, core, grp = (lax.axis_index(a) for a in ("zh", "x", "y", "core", "grp"))
    enc_place = zh * lax.axis_size("x") + x
    dec_place = y * lax.axis_size("core") + core
    dec_count = lax.axis_size("y") * lax.axis_size("core")
    slots, patch, width = images.shape[1:]
    img_rows = slots * patch
    own_rows = images.reshape(img_rows, width)
    share = fc1_weight.shape[0] // dec_count

    normed = normalize_layer(own_rows.astype(F32), ln_gain, ln_bias).astype(BF16)
    start = dec_place * share
    bias_column = lax.dynamic_slice_in_dim(fc1_bias, start, share, 0)[:, None]
    first_piece = jnp.concatenate(
        [lax.dynamic_slice_in_dim(fc1_weight, start, share, 0), three_terms(bias_column)], axis=1
    )
    second_piece = lax.dynamic_slice_in_dim(fc2_weight, start, share, 0)

    rows = gather_rel(normed, "x")
    first = gather_weight(first_piece)
    second = gather_weight(second_piece)
    query_full = lax.all_gather(query_weight, ("zh", "x"), axis=0, tiled=True)

    tile_index = jnp.arange(slots)
    own_tiles = tiles[enc_place, dec_place, grp]
    own_live = jnp.broadcast_to((tile_index < own_tiles)[:, None, None], (slots, patch, 1)).reshape(
        img_rows, 1
    )
    cotangent = jnp.where(
        own_live, state_grads.reshape(img_rows, width), jnp.zeros((), state_grads.dtype)
    )
    cotangents = gather_rel(cotangent, "x")

    bias = jnp.sum(first[:, width : width + 3].astype(F32), axis=1, keepdims=True)
    pre = (
        lax.dot_general(
            first[:, :width], rows, (((1,), (1,)), ((), ())), preferred_element_type=F32
        )
        + bias
    )
    phi = 0.5 * (1.0 + lax.erf(pre * 0.7071067811865476))
    hidden = (pre * phi).astype(BF16)
    partial_sum = lax.dot_general(
        hidden, second, (((0,), (0,)), ((), ())), preferred_element_type=F32
    ).astype(BF16)
    summed = scatter_rel(list(partial_sum.reshape(4, img_rows, width)), "x")
    states = (own_rows.astype(F32) + summed + fc2_bias).astype(BF16)

    second_term = lax.dot_general(
        hidden, cotangents, (((1,), (0,)), ((), ())), preferred_element_type=F32
    ).astype(BF16)
    hidden_grad = lax.dot_general(
        second, cotangents, (((1,), (1,)), ((), ())), preferred_element_type=F32
    )
    slope = phi + pre * jnp.exp(-0.5 * pre * pre) * 0.3989422804014327
    pre_grad = (hidden_grad * slope).astype(BF16)
    first_term = lax.dot_general(
        pre_grad, rows, (((1,), (0,)), ((), ())), preferred_element_type=F32
    ).astype(BF16)
    fc2_grad = scatter_grad(second_term)
    fc1_grad = scatter_grad(first_term)

    key_raw = jnp.dot(states, key_weight, preferred_element_type=F32).reshape(
        img_rows, KV_HEADS, HD
    )
    keys = normalize_heads(key_raw).astype(BF16)
    values = (
        jnp.dot(states, value_weight, preferred_element_type=F32)
        .astype(BF16)
        .reshape(img_rows, KV_HEADS, HD)
    )
    both = jnp.concatenate([keys, values], axis=2).transpose(1, 0, 2)
    send = jnp.broadcast_to(both[:, None], (KV_HEADS, 2, img_rows, 2 * HD)).reshape(
        dec_count, img_rows, 2 * HD
    )
    got = lax.all_to_all(send, ("y", "core"), split_axis=0, concat_axis=0, tiled=True)
    all_keys = got[:, :, :HD].reshape(dec_count * img_rows, HD)
    all_values = got[:, :, HD:].reshape(dec_count * img_rows, HD)

    samples, length = text.shape[:2]
    local_heads = query_weight.shape[1] // HD
    query_raw = jnp.dot(
        text.reshape(samples * length, text.shape[2]), query_full, preferred_element_type=F32
    )
    queries = (
        normalize_heads(query_raw.reshape(samples, length, local_heads, HD)).astype(BF16)
    ).transpose(0, 2, 1, 3)
    queries = queries.reshape(samples, local_heads * length, HD)
    dec_tiles = tiles[enc_place, :, grp]
    live_keys = tile_index[None, :] < dec_tiles[:, None]
    live_keys = jnp.broadcast_to(live_keys[:, :, None], (dec_count, slots, patch)).reshape(
        dec_count, img_rows
    )
    allowed = ((links[:, :, None] > 0) & live_keys[None, :, :]).reshape(
        samples, 1, dec_count * img_rows
    )
    scores = jnp.einsum("sqe,ke->sqk", queries, all_keys, preferred_element_type=F32) * HD ** (-0.5)
    weights = jnp.where(allowed, jnp.exp(scores), 0.0)
    totals = jnp.sum(weights, axis=-1, keepdims=True)
    probs = (weights / totals).astype(BF16)
    mixed = jnp.einsum("sqk,ke->sqe", probs, all_values, preferred_element_type=F32)
    mixed = mixed.reshape(samples, local_heads, length, HD).transpose(0, 2, 1, 3)
    valid = jnp.arange(length)[None, :] < lengths[:, None]
    context = (
        jnp.where(valid[:, :, None, None], mixed, 0.0)
        .reshape(samples, length, local_heads * HD)
        .astype(BF16)
    )
    return (context, fc1_grad, fc2_grad)


def solution(mesh):
    fine = Mesh(mesh.devices.reshape(4, 4, 4, 2, 2), ("zh", "x", "y", "core", "grp"))
    enc = ("zh", "x")
    dec = ("y", "core")
    in_specs = (
        P(enc + dec + ("grp",), None, None, None),
        P(),
        P(),
        P(enc, None),
        P(enc),
        P(enc, None),
        P(),
        P(),
        P(),
        P(enc + ("grp",), None, None),
        P(enc, dec),
        P(),
        P(enc + ("grp",), None),
        P(enc + ("grp",)),
        P(enc + dec + ("grp",), None, None, None),
    )
    out_specs = (
        P(enc + ("grp",), None, dec),
        P(enc + dec + ("grp",), None),
        P(enc + dec + ("grp",), None),
    )
    return jax.shard_map(
        on_device, mesh=fine, in_specs=in_specs, out_specs=out_specs, check_vma=False
    )
```

```python
import jax
import jax.numpy as jnp
from jax import lax
from jax.experimental import pallas as pl
from jax.experimental.pallas import tpu as pltpu
from jax.sharding import Mesh
from jax.sharding import PartitionSpec as P

HEADS = 32
KV_HEADS = 4
HD = 128
EPSILON = 1e-06
F32 = jnp.float32
BF16 = jnp.bfloat16
NT = (((1,), (1,)), ((), ()))
NN = (((1,), (0,)), ((), ()))
NX, NZ, NY, NC, NG = 4, 4, 4, 2, 2


def dot(a, b, dims):
    return lax.dot_general(a, b, dims, preferred_element_type=F32)


def local(body, outs, *args, scalars=0, raw=0, scratch=(), flops=0, limit=40, after=()):
    taken = len(args)

    def ordered(*refs):
        body(*refs[:taken], *refs[taken + len(after) :])

    moved = sum(a.size * a.dtype.itemsize for a in args)
    moved += sum(o.size * o.dtype.itemsize for o in outs)
    in_specs = [pl.BlockSpec(memory_space=pltpu.SMEM)] * scalars
    in_specs += [pl.BlockSpec(memory_space=pltpu.VMEM)] * (len(args) - scalars - raw)
    in_specs += [pl.BlockSpec(memory_space=pl.ANY)] * (raw + len(after))
    return pl.pallas_call(
        ordered,
        out_shape=tuple(outs),
        in_specs=in_specs,
        out_specs=tuple(pl.BlockSpec(memory_space=pltpu.VMEM) for _ in outs),
        scratch_shapes=scratch,
        compiler_params=pltpu.CompilerParams(vmem_limit_bytes=limit << 20),
        cost_estimate=pl.CostEstimate(flops=flops, transcendentals=0, bytes_accessed=moved),
    )(*args, *after)


def sds(shape, dtype):
    return jax.ShapeDtypeStruct(shape, dtype)


def pull(array, axis, step):
    n = lax.axis_size(axis)
    return lax.ppermute(array, axis, [((i + step) % n, i) for i in range(n)])


def push(array, axis, step):
    n = lax.axis_size(axis)
    return lax.ppermute(array, axis, [(i, (i + step) % n) for i in range(n)])


def prepare(place, x, gain, shift, grads, b1, w1, w2, both, piece, terms, sem):
    width = x.shape[1]
    share = piece.shape[0] // 2
    start = pl.multiple_of(place[0], 8)
    copies = [
        pltpu.make_async_copy(
            w.at[pl.ds(start, share), :], piece.at[pl.ds(m * share, share), pl.ds(0, width)], sem.at[m]
        )
        for m, w in enumerate((w1, w2))
    ]
    for copy in copies:
        copy.start()
    tile = x.shape[0]
    values = x[...].astype(F32)
    middle = jnp.mean(values, axis=-1, keepdims=True)
    centered = values - middle
    spread = jnp.mean(centered * centered, axis=-1, keepdims=True)
    normed = (centered * lax.rsqrt(spread + EPSILON) * gain[...] + shift[...]).astype(BF16)
    given = grads[...]
    for j in range(NX):
        both[j, :tile] = normed
        both[j, tile:] = given
    count = b1.shape[1]
    row = lax.broadcasted_iota(jnp.int32, (count, count), 0)
    lane = lax.broadcasted_iota(jnp.int32, (count, count), 1)
    column = jnp.sum(jnp.where(row == lane, b1[...], 0.0), axis=1, keepdims=True)
    first = column.astype(BF16).astype(F32)
    second = (column - first).astype(BF16).astype(F32)
    third = column - first - second
    lane = lax.broadcasted_iota(jnp.int32, terms.shape, 1)
    terms[...] = jnp.where(
        lane == 0, first, jnp.where(lane == 1, second, jnp.where(lane == 2, third, 0.0))
    ).astype(BF16)
    piece[:share, width:] = terms[pl.ds(start, share), :]
    piece[share:, width:] = jnp.zeros((share, piece.shape[1] - width), BF16)
    for copy in copies:
        copy.wait()


def join(a, b, c, out):
    n = a.shape[0]
    out[:n, :] = a[...]
    out[n : 2 * n, :] = b[...]
    out[2 * n :, :] = c[...]


def forward(place, w1, w2, terms, *refs):
    pieces, both = refs[:8], refs[8]
    hidden, slope, second, send, first, bias, whole = refs[9:]
    share = pieces[0].shape[0] // 6
    width = w1.shape[1]
    tile = both.shape[1] // 2
    for j in range(NX):
        whole[j * tile : (j + 1) * tile, :] = both[j, :tile]
    for jc in range(NC):
        for jy in range(NY):
            at = (jc * NY + jy) * NZ * share
            peer = ((place[0] + jy) % NY) * NC + (place[1] + jc) % NC
            start = pl.multiple_of(peer * share, 8)
            first[at : at + share, :] = w1[pl.ds(start, share), :]
            second[at : at + share, :] = w2[pl.ds(start, share), :]
            bias[at : at + share, :] = terms[pl.ds(start, share), :]
            piece = pieces[jc * NY + jy]
            for jz in range(1, NZ):
                to, own = at + jz * share, (jz - 1) * 2 * share
                first[to : to + share, :] = piece[own : own + share, :width]
                second[to : to + share, :] = piece[own + share : own + 2 * share, :width]
                bias[to : to + share, :] = piece[own : own + share, width:]
    count = first.shape[0]
    step = 256
    for at in range(0, count, step):
        pre = dot(first[at : at + step, :], whole[...], NT)
        pre = pre + jnp.sum(bias[at : at + step, :].astype(F32), axis=1, keepdims=True)
        phi = 0.5 * (1.0 + lax.erf(pre * 0.7071067811865476))
        hidden[at : at + step, :] = (pre * phi).astype(BF16)
        slope[at : at + step, :] = phi + pre * jnp.exp(-0.5 * pre * pre) * 0.3989422804014327
    turned = jnp.swapaxes(hidden[...], 0, 1)
    sums = dot(turned, second[...], NN).astype(BF16)
    for j in range(NX):
        send[j] = sums[j * tile : (j + 1) * tile]


def backward(live, hidden, slope, second, both, keep, send, whole, grads):
    tile, width = both.shape[1] // 2, both.shape[2]
    row = lax.broadcasted_iota(jnp.int32, (tile, width), 0)
    for j in range(NX):
        whole[j * tile : (j + 1) * tile, :] = both[j, :tile]
        given = both[j, tile:].astype(F32)
        alive = jnp.where(row < live[j] * (tile // 4), given, 0.0)
        grads[j * tile : (j + 1) * tile, :] = alive.astype(BF16)
    half = hidden.shape[0] // 2
    step = 320
    for to, base in ((send, half), (keep, 0)):
        for at in range(0, half, step):
            here = slice(base + at, base + at + step)
            to[half + at : half + at + step, :] = dot(hidden[here, :], grads[...], NN).astype(BF16)
            hidden_grad = dot(second[here, :], grads[...], NT)
            pre_grad = (hidden_grad * slope[here, :]).astype(BF16)
            to[at : at + step, :] = dot(pre_grad, whole[...], NN).astype(BF16)


def add_core(keep, got, own, send1, send2, send3):
    half = keep.shape[0] // 2
    part = half // NY
    for m in range(2):
        for j, out in enumerate((own, send1, send2, send3)):
            at = m * half + j * part
            total = keep[at : at + part, :].astype(F32) + got[at : at + part, :].astype(F32)
            out[m * part : (m + 1) * part, :] = total.astype(out.dtype)


def add_y(place, own, got1, got2, got3, out):
    half = own.shape[0] // 2
    part = half // NZ
    small = part // 2
    for m in range(2):
        for jz in range(NZ):
            here = slice(m * half + jz * part, m * half + (jz + 1) * part)
            total = own[here, :] + got1[here, :].astype(F32)
            total = total + (got2[here, :].astype(F32) + got3[here, :].astype(F32))
            to = ((place[0] + jz) % NZ) * NG
            for g in range(NG):
                block = total[g * small : (g + 1) * small].astype(BF16)
                out[to + g, m * small : (m + 1) * small, :] = block


def add_z(got, first, second):
    total = got[0].astype(F32)
    for i in range(1, got.shape[0]):
        total = total + got[i].astype(F32)
    half = total.shape[0] // 2
    first[...] = total[:half]
    second[...] = total[half:]


def project(got, x, shift, wk, wv, out):
    total = (got[0].astype(F32) + got[1].astype(F32)) + (got[2].astype(F32) + got[3].astype(F32))
    states = (x[...].astype(F32) + total + shift[...]).astype(BF16)
    keys = dot(states, wk[...], NN)
    values = dot(states, wv[...], NN).astype(BF16)
    for h in range(KV_HEADS):
        raw = keys[:, h * HD : (h + 1) * HD]
        scale = lax.rsqrt(jnp.mean(raw * raw, axis=-1, keepdims=True) + EPSILON)
        key = (raw * scale).astype(BF16)
        for c in range(NC):
            out[h * NC + c, :, :HD] = key
            out[h * NC + c, :, HD:] = values[:, h * HD : (h + 1) * HD]


def ask(text, weight, out, total):
    k = pl.program_id(0)

    @pl.when(k == 0)
    def _():
        total[...] = jnp.zeros_like(total)

    total[...] += dot(text[...], weight[...], NN)

    @pl.when(k == pl.num_programs(0) - 1)
    def _():
        for h in range(out.shape[1] // HD):
            raw = total[:, h * HD : (h + 1) * HD]
            scale = lax.rsqrt(jnp.mean(raw * raw, axis=-1, keepdims=True) + EPSILON)
            out[:, h * HD : (h + 1) * HD] = (raw * scale).astype(BF16)


def attend(tiles, links, lengths, queries, got, out):
    samples, length, width = out.shape
    heads = width // HD
    images, img_rows = got.shape[:2]
    lane = lax.broadcasted_iota(jnp.int32, (1, 2 * img_rows), 1)
    position = lax.broadcasted_iota(jnp.int32, (length, HD), 0)
    for s in range(samples):
        mine = queries[s * length : (s + 1) * length, :]
        asked = jnp.concatenate([mine[:, h * HD : (h + 1) * HD] for h in range(heads)], axis=0)
        total = jnp.zeros((heads * length, 1), F32)
        mixed = jnp.zeros((heads * length, HD), F32)
        for j in range(0, images, 2):
            keys = jnp.concatenate([got[j, :, :HD], got[j + 1, :, :HD]], axis=0)
            values = jnp.concatenate([got[j, :, HD:], got[j + 1, :, HD:]], axis=0)
            scores = dot(asked, keys, NT) * HD ** (-0.5)
            reach0 = tiles[j] * (img_rows // 4) * links[s, j]
            reach1 = tiles[j + 1] * (img_rows // 4) * links[s, j + 1]
            reach = jnp.where(lane < img_rows, reach0, img_rows + reach1)
            weights = jnp.exp(scores) * jnp.where(lane < reach, 1.0, 0.0)
            total = total + jnp.sum(weights, axis=-1, keepdims=True)
            mixed = mixed + dot(weights.astype(BF16), values, NN)
        mixed = mixed / total
        valid = position < lengths[s]
        for h in range(heads):
            part = jnp.where(valid, mixed[h * length : (h + 1) * length, :], 0.0)
            out[s, :, h * HD : (h + 1) * HD] = part.astype(BF16)


def on_device(
    images,
    ln_gain,
    ln_bias,
    fc1_weight,
    fc1_bias,
    fc2_weight,
    fc2_bias,
    key_weight,
    value_weight,
    text,
    query_weight,
    tiles,
    links,
    lengths,
    state_grads,
):
    zh, x, y, core, grp = (lax.axis_index(a) for a in ("zh", "x", "y", "core", "grp"))
    enc_place = zh * NX + x
    dec_place = y * NC + core
    dec_count = NY * NC
    slots, patch, width = images.shape[1:]
    img_rows = slots * patch
    own_rows = images.reshape(img_rows, width)
    shard = fc1_weight.shape[0]
    share = shard // dec_count
    count = shard * NZ
    wide = width + HD

    spread_rows, piece, terms = local(
        prepare,
        [
            sds((NX, 2 * img_rows, width), BF16),
            sds((2 * share, wide), BF16),
            sds((shard, HD), BF16),
        ],
        (dec_place * share)[None],
        own_rows,
        ln_gain[None],
        ln_bias[None],
        state_grads.reshape(img_rows, width),
        fc1_bias[None],
        fc1_weight,
        fc2_weight,
        scalars=1,
        raw=2,
        scratch=[pltpu.SemaphoreType.DMA((2,))],
    )
    from_zh = [pull(piece, "zh", j) for j in range(1, NZ)]
    rows = lax.all_to_all(spread_rows, "x", split_axis=0, concat_axis=0, tiled=True)
    (joined,) = local(join, [sds((6 * share, wide), BF16)], *from_zh, after=[rows])
    late_weight, *_ = lax.optimization_barrier((query_weight, joined))
    query_full = lax.all_gather(late_weight, ("zh", "x"), axis=0, tiled=True)
    near = [joined] + [pull(joined, "y", j) for j in range(1, NY)]
    pieces = near + [pull(p, "core", 1) for p in near]

    hidden, slope, second, sends = local(
        forward,
        [
            sds((count, NX * img_rows), BF16),
            sds((count, NX * img_rows), F32),
            sds((count, width), BF16),
            sds((NX, img_rows, width), BF16),
        ],
        jnp.stack([y, core]),
        fc1_weight,
        fc2_weight,
        terms,
        *pieces,
        rows,
        scalars=1,
        scratch=[
            pltpu.VMEM((count, width), BF16),
            pltpu.VMEM((count, HD), BF16),
            pltpu.VMEM((NX * img_rows, width), BF16),
        ],
        flops=4 * count * NX * img_rows * width,
        limit=50,
    )
    sums = lax.all_to_all(sends, "x", split_axis=0, concat_axis=0, tiled=True)
    live = lax.dynamic_slice(tiles, (zh * NX, dec_place, grp), (NX, 1, 1)).reshape(NX)

    half = count // 2
    g_keep, g_send = local(
        backward,
        [sds((count, width), BF16), sds((count, width), BF16)],
        live,
        hidden,
        slope,
        second,
        rows,
        scalars=1,
        scratch=[
            pltpu.VMEM((NX * img_rows, width), BF16),
            pltpu.VMEM((NX * img_rows, width), BF16),
        ],
        flops=6 * count * NX * img_rows * width,
        limit=50,
    )
    (send,) = local(
        project,
        [sds((dec_count, img_rows, 2 * HD), BF16)],
        sums,
        own_rows,
        fc2_bias[None],
        key_weight,
        value_weight,
        flops=4 * img_rows * width * KV_HEADS * HD,
    )
    got = lax.all_to_all(send, ("y", "core"), split_axis=0, concat_axis=0, tiled=True)

    g_got = push(g_send, "core", 1)
    part = count // NY
    y_own, *y_sends = local(
        add_core,
        [sds((part, width), F32)] + [sds((part, width), BF16)] * 3,
        g_keep,
        g_got,
        after=[send],
    )
    y_got = [push(y_sends[j - 1], "y", j) for j in range(1, NY)]
    samples, length, deep = text.shape
    mine = query_weight.shape[1]
    grid = 8
    queries = pl.pallas_call(
        ask,
        grid=(grid,),
        in_specs=[
            pl.BlockSpec((samples * length, deep // grid), lambda k: (0, k)),
            pl.BlockSpec((deep // grid, mine), lambda k: (k, 0)),
        ],
        out_specs=pl.BlockSpec((samples * length, mine), lambda k: (0, 0)),
        out_shape=sds((samples * length, mine), BF16),
        scratch_shapes=[pltpu.VMEM((samples * length, mine), F32)],
        compiler_params=pltpu.CompilerParams(vmem_limit_bytes=24 << 20),
        cost_estimate=pl.CostEstimate(
            flops=2 * samples * length * deep * mine,
            transcendentals=0,
            bytes_accessed=2 * deep * (samples * length + mine),
        ),
    )(text.reshape(samples * length, deep), query_full)
    (z_send,) = local(
        add_y,
        [sds((NZ * NG, share, width), BF16)],
        zh[None],
        y_own,
        *y_got,
        scalars=1,
        after=[queries],
    )
    z_got = lax.all_to_all(z_send, ("zh", "grp"), split_axis=0, concat_axis=0, tiled=True)
    (context,) = local(
        attend,
        [sds((samples, length, mine), BF16)],
        tiles[enc_place, :, grp],
        links,
        lengths,
        queries,
        got,
        scalars=3,
        flops=4 * samples * length * mine * dec_count * img_rows,
    )
    fc1_grad, fc2_grad = local(
        add_z, [sds((share // 2, width), F32)] * 2, z_got, after=[context]
    )
    return (context, fc1_grad, fc2_grad)


def solution(mesh):
    fine = Mesh(mesh.devices.reshape(NZ, NX, NY, NC, NG), ("zh", "x", "y", "core", "grp"))
    enc = ("zh", "x")
    dec = ("y", "core")
    in_specs = (
        P(enc + dec + ("grp",), None, None, None),
        P(),
        P(),
        P(enc, None),
        P(enc),
        P(enc, None),
        P(),
        P(),
        P(),
        P(enc + ("grp",), None, None),
        P(enc, dec),
        P(),
        P(enc + ("grp",), None),
        P(enc + ("grp",)),
        P(enc + dec + ("grp",), None, None, None),
    )
    out_specs = (
        P(enc + ("grp",), None, dec),
        P(enc + dec + ("grp",), None),
        P(enc + dec + ("grp",), None),
    )
    return jax.shard_map(
        on_device, mesh=fine, in_specs=in_specs, out_specs=out_specs, check_vma=False
    )
```

```python
import jax
import jax.numpy as jnp
from jax import lax
from jax.experimental import pallas as pl
from jax.experimental.pallas import tpu as pltpu
from jax.sharding import Mesh
from jax.sharding import PartitionSpec as P

HEADS = 32
KV_HEADS = 4
HD = 128
EPSILON = 1e-06
F32 = jnp.float32
BF16 = jnp.bfloat16
NT = (((1,), (1,)), ((), ()))
NN = (((1,), (0,)), ((), ()))
NX, NZ, NY, NC, NG = 4, 4, 4, 2, 2


def dot(a, b, dims):
    return lax.dot_general(a, b, dims, preferred_element_type=F32)


def local(body, outs, *args, scalars=0, raw=0, scratch=(), flops=0, limit=40, after=()):
    taken = len(args)

    def ordered(*refs):
        body(*refs[:taken], *refs[taken + len(after) :])

    moved = sum(a.size * a.dtype.itemsize for a in args)
    moved += sum(o.size * o.dtype.itemsize for o in outs)
    in_specs = [pl.BlockSpec(memory_space=pltpu.SMEM)] * scalars
    in_specs += [pl.BlockSpec(memory_space=pltpu.VMEM)] * (len(args) - scalars - raw)
    in_specs += [pl.BlockSpec(memory_space=pltpu.MemorySpace.HBM)] * raw
    in_specs += [pl.BlockSpec(memory_space=pl.ANY)] * len(after)
    return pl.pallas_call(
        ordered,
        out_shape=tuple(outs),
        in_specs=in_specs,
        out_specs=tuple(pl.BlockSpec(memory_space=pltpu.VMEM) for _ in outs),
        scratch_shapes=scratch,
        compiler_params=pltpu.CompilerParams(vmem_limit_bytes=limit << 20),
        cost_estimate=pl.CostEstimate(flops=flops, transcendentals=0, bytes_accessed=moved),
    )(*args, *after)


def sds(shape, dtype):
    return jax.ShapeDtypeStruct(shape, dtype)


def pull(array, axis, step):
    n = lax.axis_size(axis)
    return lax.ppermute(array, axis, [((i + step) % n, i) for i in range(n)])


def push(array, axis, step):
    n = lax.axis_size(axis)
    return lax.ppermute(array, axis, [(i, (i + step) % n) for i in range(n)])


def prepare(place, gain, shift, b1, images, grads, w1, w2, both, piece, terms, x, sem):
    tile, width = x.shape
    share = piece.shape[0] // 2
    start = pl.multiple_of(place[0], 8)
    first_in = pltpu.make_async_copy(images, x, sem.at[0])
    first_in.start()
    copies = [
        pltpu.make_async_copy(
            w.at[pl.ds(start, share), :],
            piece.at[pl.ds(m * share, share), pl.ds(0, width)],
            sem.at[1 + m],
        )
        for m, w in enumerate((w1, w2))
    ]
    copies += [
        pltpu.make_async_copy(grads, both.at[j, pl.ds(tile, tile), :], sem.at[3 + j])
        for j in range(NX)
    ]
    for copy in copies:
        copy.start()
    count = b1.shape[1]
    row = lax.broadcasted_iota(jnp.int32, (count, count), 0)
    lane = lax.broadcasted_iota(jnp.int32, (count, count), 1)
    column = jnp.sum(jnp.where(row == lane, b1[...], 0.0), axis=1, keepdims=True)
    first = column.astype(BF16).astype(F32)
    second = (column - first).astype(BF16).astype(F32)
    third = column - first - second
    lane = lax.broadcasted_iota(jnp.int32, terms.shape, 1)
    terms[...] = jnp.where(
        lane == 0, first, jnp.where(lane == 1, second, jnp.where(lane == 2, third, 0.0))
    ).astype(BF16)
    piece[:share, width:] = terms[pl.ds(start, share), :]
    piece[share:, width:] = jnp.zeros((share, piece.shape[1] - width), BF16)
    first_in.wait()
    values = x[...].astype(F32)
    middle = jnp.mean(values, axis=-1, keepdims=True)
    centered = values - middle
    spread = jnp.mean(centered * centered, axis=-1, keepdims=True)
    normed = (centered * lax.rsqrt(spread + EPSILON) * gain[...] + shift[...]).astype(BF16)
    for j in range(NX):
        both[j, :tile] = normed
    for copy in copies:
        copy.wait()


def join(a, b, c, out):
    n = a.shape[0]
    out[:n, :] = a[...]
    out[n : 2 * n, :] = b[...]
    out[2 * n :, :] = c[...]


def mlp(place, live, w1, w2, terms, *refs):
    pieces, mine, other = refs[:4], refs[4], refs[5]
    send, own, out1, out2, out3 = refs[6:11]
    first, second, bias, whole, grads, hidden, slope = refs[11:]
    share = pieces[0].shape[0] // 6
    width = w1.shape[1]
    tile = mine.shape[1] // 2
    row = lax.broadcasted_iota(jnp.int32, (tile, width), 0)
    for c, both in enumerate((mine, other)):
        for j in range(NX):
            here = slice((c * NX + j) * tile, (c * NX + j + 1) * tile)
            whole[here, :] = both[j, :tile]
            given = both[j, tile:].astype(F32)
            alive = jnp.where(row < live[c * NX + j] * (tile // 4), given, 0.0)
            grads[here, :] = alive.astype(BF16)
    for jy in range(NY):
        at = jy * NZ * share
        peer = ((place[0] + jy) % NY) * NC + place[1]
        start = pl.multiple_of(peer * share, 8)
        first[at : at + share, :] = w1[pl.ds(start, share), :]
        second[at : at + share, :] = w2[pl.ds(start, share), :]
        bias[at : at + share, :] = terms[pl.ds(start, share), :]
        piece = pieces[jy]
        for jz in range(1, NZ):
            to, from_ = at + jz * share, (jz - 1) * 2 * share
            first[to : to + share, :] = piece[from_ : from_ + share, :width]
            second[to : to + share, :] = piece[from_ + share : from_ + 2 * share, :width]
            bias[to : to + share, :] = piece[from_ : from_ + share, width:]
    count = first.shape[0]
    step = count // NY
    for at in range(0, count, step):
        pre = dot(first[at : at + step, :], whole[...], NT)
        pre = pre + jnp.sum(bias[at : at + step, :].astype(F32), axis=1, keepdims=True)
        phi = 0.5 * (1.0 + lax.erf(pre * 0.7071067811865476))
        hidden[at : at + step, :] = (pre * phi).astype(BF16)
        slope[at : at + step, :] = phi + pre * jnp.exp(-0.5 * pre * pre) * 0.3989422804014327
    turned = jnp.swapaxes(hidden[...], 0, 1)
    for c in range(NC):
        for j in range(NX):
            here = slice((c * NX + j) * tile, (c * NX + j + 1) * tile)
            part = dot(turned[here], second[...], NN).astype(BF16)
            send[j * NC + (place[1] + c) % NC] = part
    for jy, out in enumerate((own, out1, out2, out3)):
        here = slice(jy * step, (jy + 1) * step)
        out[step:, :] = dot(hidden[here, :], grads[...], NN).astype(out.dtype)
        pre_grad = (dot(second[here, :], grads[...], NT) * slope[here, :]).astype(BF16)
        out[:step, :] = dot(pre_grad, whole[...], NN).astype(out.dtype)


def add_y(place, own, got1, got2, got3, out):
    half = own.shape[0] // 2
    part = half // NZ
    small = part // 2
    for m in range(2):
        for jz in range(NZ):
            here = slice(m * half + jz * part, m * half + (jz + 1) * part)
            total = own[here, :] + got1[here, :].astype(F32)
            total = total + (got2[here, :].astype(F32) + got3[here, :].astype(F32))
            to = ((place[0] + jz) % NZ) * NG
            for g in range(NG):
                block = total[g * small : (g + 1) * small].astype(BF16)
                out[to + g, m * small : (m + 1) * small, :] = block


def add_z(got, first, second):
    total = got[0].astype(F32)
    for i in range(1, got.shape[0]):
        total = total + got[i].astype(F32)
    half = total.shape[0] // 2
    first[...] = total[:half]
    second[...] = total[half:]


def project(got, x, shift, wk, wv, out):
    total = got[0].astype(F32)
    for i in range(1, got.shape[0]):
        total = total + got[i].astype(F32)
    states = (x[...].astype(F32) + total + shift[...]).astype(BF16)
    keys = dot(states, wk[...], NN)
    values = dot(states, wv[...], NN).astype(BF16)
    for h in range(KV_HEADS):
        raw = keys[:, h * HD : (h + 1) * HD]
        scale = lax.rsqrt(jnp.mean(raw * raw, axis=-1, keepdims=True) + EPSILON)
        key = (raw * scale).astype(BF16)
        for c in range(NC):
            out[h * NC + c, :, :HD] = key
            out[h * NC + c, :, HD:] = values[:, h * HD : (h + 1) * HD]


def ask(text, weight, out, total):
    k = pl.program_id(0)

    @pl.when(k == 0)
    def _():
        total[...] = jnp.zeros_like(total)

    total[...] += dot(text[...], weight[...], NN)

    @pl.when(k == pl.num_programs(0) - 1)
    def _():
        for h in range(out.shape[1] // HD):
            raw = total[:, h * HD : (h + 1) * HD]
            scale = lax.rsqrt(jnp.mean(raw * raw, axis=-1, keepdims=True) + EPSILON)
            out[:, h * HD : (h + 1) * HD] = (raw * scale).astype(BF16)


def attend(tiles, links, lengths, queries, got, out):
    samples, length, width = out.shape
    heads = width // HD
    images, img_rows = got.shape[:2]
    lane = lax.broadcasted_iota(jnp.int32, (1, 2 * img_rows), 1)
    position = lax.broadcasted_iota(jnp.int32, (length, HD), 0)
    for s in range(samples):
        mine = queries[s * length : (s + 1) * length, :]
        asked = jnp.concatenate([mine[:, h * HD : (h + 1) * HD] for h in range(heads)], axis=0)
        total = jnp.zeros((heads * length, 1), F32)
        mixed = jnp.zeros((heads * length, HD), F32)
        for j in range(0, images, 2):
            keys = jnp.concatenate([got[j, :, :HD], got[j + 1, :, :HD]], axis=0)
            values = jnp.concatenate([got[j, :, HD:], got[j + 1, :, HD:]], axis=0)
            scores = dot(asked, keys, NT) * HD ** (-0.5)
            reach0 = tiles[j] * (img_rows // 4) * links[s, j]
            reach1 = tiles[j + 1] * (img_rows // 4) * links[s, j + 1]
            reach = jnp.where(lane < img_rows, reach0, img_rows + reach1)
            weights = jnp.exp(scores) * jnp.where(lane < reach, 1.0, 0.0)
            total = total + jnp.sum(weights, axis=-1, keepdims=True)
            mixed = mixed + dot(weights.astype(BF16), values, NN)
        mixed = mixed / total
        valid = position < lengths[s]
        for h in range(heads):
            part = jnp.where(valid, mixed[h * length : (h + 1) * length, :], 0.0)
            out[s, :, h * HD : (h + 1) * HD] = part.astype(BF16)


def on_device(
    images,
    ln_gain,
    ln_bias,
    fc1_weight,
    fc1_bias,
    fc2_weight,
    fc2_bias,
    key_weight,
    value_weight,
    text,
    query_weight,
    tiles,
    links,
    lengths,
    state_grads,
):
    zh, x, y, core, grp = (lax.axis_index(a) for a in ("zh", "x", "y", "core", "grp"))
    enc_place = zh * NX + x
    dec_place = y * NC + core
    dec_count = NY * NC
    slots, patch, width = images.shape[1:]
    img_rows = slots * patch
    own_rows = images.reshape(img_rows, width)
    shard = fc1_weight.shape[0]
    share = shard // dec_count
    wide = width + HD

    spread_rows, piece, terms = local(
        prepare,
        [
            sds((NX, 2 * img_rows, width), BF16),
            sds((2 * share, wide), BF16),
            sds((shard, HD), BF16),
        ],
        (dec_place * share)[None],
        ln_gain[None],
        ln_bias[None],
        fc1_bias[None],
        own_rows,
        state_grads.reshape(img_rows, width),
        fc1_weight,
        fc2_weight,
        scalars=1,
        raw=4,
        scratch=[pltpu.VMEM((img_rows, width), BF16), pltpu.SemaphoreType.DMA((3 + NX,))],
    )
    from_zh = [pull(piece, "zh", j) for j in range(1, NZ)]
    rows = lax.all_to_all(spread_rows, "x", split_axis=0, concat_axis=0, tiled=True)
    (joined,) = local(join, [sds((6 * share, wide), BF16)], *from_zh, after=[rows])
    late_weight, *_ = lax.optimization_barrier((query_weight, joined))
    query_full = lax.all_gather(late_weight, ("zh", "x"), axis=0, tiled=True)
    pieces = [joined] + [pull(joined, "y", j) for j in range(1, NY)]
    other_rows = pull(rows, "core", 1)

    column = lax.dynamic_slice(tiles, (zh * NX, 0, grp), (NX, dec_count, 1))
    column = column.reshape(NX, NY, NC)
    near = lax.dynamic_slice_in_dim(column, y, 1, 1)[:, 0]
    live = jnp.concatenate(
        [
            lax.dynamic_slice_in_dim(near, core, 1, 1)[:, 0],
            lax.dynamic_slice_in_dim(near, 1 - core, 1, 1)[:, 0],
        ]
    )
    count = shard * NZ // NC
    total_rows = NX * NC * img_rows
    part = 2 * count // NY
    sends, y_own, *y_sends = local(
        mlp,
        [
            sds((NX * NC, img_rows, width), BF16),
            sds((part, width), F32),
        ]
        + [sds((part, width), BF16)] * 3,
        jnp.stack([y, core]),
        live,
        fc1_weight,
        fc2_weight,
        terms,
        *pieces,
        rows,
        other_rows,
        scalars=2,
        scratch=[
            pltpu.VMEM((count, width), BF16),
            pltpu.VMEM((count, width), BF16),
            pltpu.VMEM((count, HD), BF16),
            pltpu.VMEM((total_rows, width), BF16),
            pltpu.VMEM((total_rows, width), BF16),
            pltpu.VMEM((count, total_rows), BF16),
            pltpu.VMEM((count, total_rows), F32),
        ],
        flops=10 * count * total_rows * width,
        limit=50,
    )
    y_got = [push(y_sends[j - 1], "y", j) for j in range(1, NY)]
    sums = lax.all_to_all(sends, ("x", "core"), split_axis=0, concat_axis=0, tiled=True)
    (send,) = local(
        project,
        [sds((dec_count, img_rows, 2 * HD), BF16)],
        sums,
        own_rows,
        fc2_bias[None],
        key_weight,
        value_weight,
        flops=4 * img_rows * width * KV_HEADS * HD,
    )
    got = lax.all_to_all(send, ("y", "core"), split_axis=0, concat_axis=0, tiled=True)

    samples, length, deep = text.shape
    mine = query_weight.shape[1]
    grid = 8
    queries = pl.pallas_call(
        ask,
        grid=(grid,),
        in_specs=[
            pl.BlockSpec((samples * length, deep // grid), lambda k: (0, k)),
            pl.BlockSpec((deep // grid, mine), lambda k: (k, 0)),
        ],
        out_specs=pl.BlockSpec((samples * length, mine), lambda k: (0, 0)),
        out_shape=sds((samples * length, mine), BF16),
        scratch_shapes=[pltpu.VMEM((samples * length, mine), F32)],
        compiler_params=pltpu.CompilerParams(vmem_limit_bytes=24 << 20),
        cost_estimate=pl.CostEstimate(
            flops=2 * samples * length * deep * mine,
            transcendentals=0,
            bytes_accessed=2 * deep * (samples * length + mine),
        ),
    )(text.reshape(samples * length, deep), query_full)
    (z_send,) = local(
        add_y,
        [sds((NZ * NG, share, width), BF16)],
        zh[None],
        y_own,
        *y_got,
        scalars=1,
    )
    z_got = lax.all_to_all(z_send, ("zh", "grp"), split_axis=0, concat_axis=0, tiled=True)
    (context,) = local(
        attend,
        [sds((samples, length, mine), BF16)],
        tiles[enc_place, :, grp],
        links,
        lengths,
        queries,
        got,
        scalars=3,
        flops=4 * samples * length * mine * dec_count * img_rows,
    )
    fc1_grad, fc2_grad = local(
        add_z, [sds((share // 2, width), F32)] * 2, z_got, after=[context]
    )
    return (context, fc1_grad, fc2_grad)


def solution(mesh):
    fine = Mesh(mesh.devices.reshape(NZ, NX, NY, NC, NG), ("zh", "x", "y", "core", "grp"))
    enc = ("zh", "x")
    dec = ("y", "core")
    in_specs = (
        P(enc + dec + ("grp",), None, None, None),
        P(),
        P(),
        P(enc, None),
        P(enc),
        P(enc, None),
        P(),
        P(),
        P(),
        P(enc + ("grp",), None, None),
        P(enc, dec),
        P(),
        P(enc + ("grp",), None),
        P(enc + ("grp",)),
        P(enc + dec + ("grp",), None, None, None),
    )
    out_specs = (
        P(enc + ("grp",), None, dec),
        P(enc + dec + ("grp",), None),
        P(enc + dec + ("grp",), None),
    )
    return jax.shard_map(
        on_device, mesh=fine, in_specs=in_specs, out_specs=out_specs, check_vma=False
    )
```
